256 devices in a mesh: frame: 16 (over x_hi, z), head: 8 (over y, core), dp: 2 (over x_lo).
Axes of the slice: x: 4 (x_hi: 2, x_lo: 2; x = x_hi * 2 + x_lo), y: 4, z: 8, core: 2. Of those that a mesh axis runs over, the one named last changes fastest.
Arguments:
- clip: bfloat16 [2, 4096, 256], P('dp', 'frame'), may hold values from -40 to 40
- block_ids: int32 [2, 4096], P('dp'), may hold values from 0 to 63, never falling along the last dimension, each value on 1 to 128 neighbouring positions
- w_spatial: bfloat16 [9, 256, 256], replicated, may hold values from -0.125 to 0.125
- w_temporal: bfloat16 [3, 256, 256], replicated, may hold values from -0.21875 to 0.21875
- w_query: bfloat16 [256, 2048], P(None, 'head'), may hold values from -0.375 to 0.375
- w_key: bfloat16 [256, 2048], P(None, 'head'), may hold values from -0.375 to 0.375
- w_value: bfloat16 [256, 2048], P(None, 'head'), may hold values from -0.375 to 0.375
- w_out: bfloat16 [2048, 256], P('head'), may hold values from -0.125 to 0.125
- cotangent: bfloat16 [2, 4096, 256], P('dp', 'frame'), may hold values from -6 to 6
Outputs:
- grad_spatial: float32 [9, 256, 256], replicated
- grad_temporal: float32 [3, 256, 256], replicated
- grad_query: float32 [256, 2048], P(None, 'head')
- grad_key: float32 [256, 2048], P(None, 'head')
- grad_value: float32 [256, 2048], P(None, 'head')
- grad_out: float32 [2048, 256], P('head')
The draws below stay inside these ranges and needn't reach their ends.
Inputs may be any that keep to these rules, and one draw needn't show every extreme that they name: `block_ids`: block numbers never fall along a clip's tokens; every block has 1 to (128) tokens.
All inputs are finite; a program needn't handle non-finite values.
Results may differ from the reference program's by a relative error of at most 0.04.
Values may be sent and summed in bfloat16 or wider, within the bound.
No kernel may reach another device: no remote copies, remote signals or barrier semaphores. Data moves between devices by JAX's collectives and lax.ppermute only.
A program may use at most 128 MiB of HBM per device.

```python
import math
import jax
import jax.numpy as jnp
import numpy as np
from jax import lax

C = 256
HEADS = 16
HD = 128
SIDE = 8
FRAMES = 64
TOKENS = 4096
CLIPS = 2


def draw_clip(key, part):
    first_key = jax.random.fold_in(key, 0)
    shape = (CLIPS, TOKENS, C)
    values = jax.random.normal(first_key, shape, jnp.float32)
    return jnp.clip(values, -40.0, 40.0).astype(jnp.bfloat16)


def block_scale(key, shape, cuts, smallest, high):
    loudness, own = 1.0, jax.random.fold_in(key, 6)
    for dim, parts in cuts:
        steps = jnp.exp(jax.random.uniform(jax.random.fold_in(own, dim), (parts,), jnp.float32, smallest / len(cuts), high / len(cuts)))
        loudness = loudness * jnp.repeat(steps, shape[dim] // parts).reshape([-1 if axis == dim else 1 for axis in range(len(shape))])
    return loudness


def profile(amount, total, limit, skew):
    loads = [(1 << 20) // math.isqrt(rank ** skew) + 1 for rank in range(2, amount + 1)]
    spare, given = total - limit - (amount - 1), [1] * (amount - 1)
    while spare > 0:
        candidates = [i for i in range(amount - 1) if given[i] < limit]
        pool, budget = sum([loads[i] for i in candidates]), spare
        for i in candidates:
            extra = min(limit - given[i], max(1, budget * loads[i] // pool), spare)
            given[i] = given[i] + extra
            spare = spare - extra
    return np.array([limit] + given)


def uneven(own_key, count, total, most, slope):
    if count == 2:
        one = jax.random.randint(own_key, (), max(1, total - most), min(most, total - 1) + 1)
        return jnp.stack([one, total - one])
    tallies = jnp.asarray(profile(count, total, most, slope), jnp.int32)
    pairs = (count - 1) // 2
    giver, sink = tallies[1:1 + 2 * pairs:2], tallies[2:2 + 2 * pairs:2]
    margin = jnp.minimum(giver - 1, most - sink)
    moved = jax.random.randint(jax.random.fold_in(own_key, 1), (pairs,), 0, 1 << 20) % (margin + 1)
    tallies = tallies.at[1:1 + 2 * pairs:2].set(giver - moved).at[2:2 + 2 * pairs:2].set(sink + moved)
    return tallies[jax.random.permutation(jax.random.fold_in(own_key, 2), count)]


def gaussian(own_key, shape, spread, bound, pieces=(), dtype=jnp.bfloat16):
    result = jax.random.normal(own_key, shape, jnp.float32) * spread
    if len(pieces) > 0:
        result = block_scale(own_key, shape, pieces, -0.22, 0.18) * result
    return jnp.clip(result, min=-bound, max=bound).astype(dtype)


def setup_inputs(seed: int = 0) -> dict:
    key_of = jax.random.split(jax.random.key(seed), 10)
    clip = draw_clip(jax.random.fold_in(key_of[9], 71), 0)
    block_ids = jax.vmap(lambda own: jnp.searchsorted(jnp.cumsum(uneven(own, FRAMES, TOKENS, 2 * SIDE * SIDE, 1)), jnp.arange(TOKENS), side="right"))(jax.random.split(key_of[1], CLIPS)).reshape((CLIPS, TOKENS)).astype(jnp.int32)
    w_spatial = gaussian(key_of[2], (9, C, C), (9 * C) ** -0.5, 0.125)
    w_temporal = gaussian(key_of[3], (3, C, C), (3 * C) ** -0.5, 0.21875)
    w_query = gaussian(key_of[4], (C, HEADS * HD), C ** -0.5, 0.375, ((1, 8),))
    w_key = gaussian(key_of[5], (C, HEADS * HD), C ** -0.5, 0.375, ((1, 8),))
    w_value = gaussian(key_of[6], (C, HEADS * HD), C ** -0.5, 0.375, ((1, 8),))
    w_out = gaussian(key_of[7], (HEADS * HD, C), (HEADS * HD) ** -0.5, 0.125, ((0, 8),))
    cotangent = gaussian(key_of[8], (CLIPS, TOKENS, C), 1.0, 6.0, ((0, 2), (1, 16)))
    return {"clip": clip, "block_ids": block_ids, "w_spatial": w_spatial, "w_temporal": w_temporal, "w_query": w_query, "w_key": w_key, "w_value": w_value, "w_out": w_out, "cotangent": cotangent}


NEG_FILL = -1.0e30


def spatial_taps(frame_grid, side):
    padded = jnp.pad(frame_grid, ((0, 0), (1, 1), (1, 1), (0, 0)))
    count = frame_grid.shape[0] * side * side
    width = frame_grid.shape[3]
    return [padded[:, row_off:row_off + side, col_off:col_off + side, :].reshape(count, width) for row_off in range(3) for col_off in range(3)]


def silu_slope(pre_act):
    sigma = jax.nn.sigmoid(pre_act)
    return sigma * (1.0 + pre_act * (1.0 - sigma))


def head_pass(operands, visible):
    query_head, key_head, value_head, grad_head = operands
    scale = HD ** -0.5
    scores = jnp.dot(query_head, key_head.T, preferred_element_type=jnp.float32) * scale
    masked = jnp.where(visible, scores, NEG_FILL)
    top = jnp.max(masked, axis=1, keepdims=True)
    total = jnp.sum(jnp.where(visible, jnp.exp(masked - top), 0.0), axis=1, keepdims=True)
    log_norm = top + jnp.log(total)
    probs = jnp.where(visible, jnp.exp(masked - log_norm), 0.0)
    probs_low = probs.astype(jnp.bfloat16)
    attended = jnp.dot(probs_low, value_head, preferred_element_type=jnp.float32).astype(jnp.bfloat16)
    delta = jnp.sum(grad_head.astype(jnp.float32) * attended.astype(jnp.float32), axis=1, keepdims=True)
    grad_probs = jnp.dot(grad_head, value_head.T, preferred_element_type=jnp.float32)
    grad_scores = (probs * (grad_probs - delta) * scale).astype(jnp.bfloat16)
    grad_query = jnp.dot(grad_scores, key_head, preferred_element_type=jnp.float32).astype(jnp.bfloat16)
    grad_key = jnp.dot(grad_scores.T, query_head, preferred_element_type=jnp.float32).astype(jnp.bfloat16)
    grad_value = jnp.dot(probs_low.T, grad_head, preferred_element_type=jnp.float32).astype(jnp.bfloat16)
    return attended, grad_query, grad_key, grad_value


def one_clip(frames_in, clip_blocks, upstream, w_spatial, w_temporal, w_query, w_key, w_value, w_out):
    tokens_all, channels = frames_in.shape
    frame_len = SIDE * SIDE
    grid = frames_in.reshape(FRAMES, SIDE, SIDE, channels)
    taps = spatial_taps(grid, SIDE)
    pre_act = jnp.zeros((tokens_all, channels), jnp.float32)
    for offset in range(9):
        pre_act = pre_act + jnp.dot(taps[offset], w_spatial[offset], preferred_element_type=jnp.float32)
    hidden = jax.nn.silu(pre_act).astype(jnp.bfloat16)
    hidden_pad = jnp.pad(hidden, ((frame_len, frame_len), (0, 0)))
    temporal = jnp.zeros((tokens_all, channels), jnp.float32)
    for offset in range(3):
        temporal = temporal + jnp.dot(hidden_pad[offset * frame_len:offset * frame_len + tokens_all], w_temporal[offset], preferred_element_type=jnp.float32)
    features = temporal.astype(jnp.bfloat16)
    queries = jnp.dot(features, w_query, preferred_element_type=jnp.float32).astype(jnp.bfloat16)
    keys_all = jnp.dot(features, w_key, preferred_element_type=jnp.float32).astype(jnp.bfloat16)
    values_all = jnp.dot(features, w_value, preferred_element_type=jnp.float32).astype(jnp.bfloat16)
    grad_attended = jnp.dot(upstream, w_out.T, preferred_element_type=jnp.float32).astype(jnp.bfloat16)
    visible = clip_blocks[None, :] <= clip_blocks[:, None]

    def split_heads(matrix):
        return matrix.reshape(tokens_all, HEADS, HD).transpose(1, 0, 2)

    def join_heads(stacked):
        return stacked.transpose(1, 0, 2).reshape(tokens_all, HEADS * HD)

    def run_head(operands):
        return head_pass(operands, visible)

    results = lax.map(run_head, (split_heads(queries), split_heads(keys_all), split_heads(values_all), split_heads(grad_attended)))
    attended, grad_queries, grad_keys, grad_values = [join_heads(item) for item in results]
    grad_wo = jnp.dot(attended.T, upstream, preferred_element_type=jnp.float32)
    grad_wq = jnp.dot(features.T, grad_queries, preferred_element_type=jnp.float32)
    grad_wk = jnp.dot(features.T, grad_keys, preferred_element_type=jnp.float32)
    grad_wv = jnp.dot(features.T, grad_values, preferred_element_type=jnp.float32)
    back_sum = jnp.dot(grad_queries, w_query.T, preferred_element_type=jnp.float32)
    back_sum = back_sum + jnp.dot(grad_keys, w_key.T, preferred_element_type=jnp.float32)
    back_sum = back_sum + jnp.dot(grad_values, w_value.T, preferred_element_type=jnp.float32)
    grad_features = (back_sum + upstream.astype(jnp.float32)).astype(jnp.bfloat16)
    grad_pad = jnp.pad(grad_features, ((frame_len, frame_len), (0, 0)))
    grad_wt = jnp.stack([jnp.dot(hidden_pad[offset * frame_len:offset * frame_len + tokens_all].T, grad_features, preferred_element_type=jnp.float32) for offset in range(3)])
    grad_hidden = jnp.zeros((tokens_all, channels), jnp.float32)
    for offset in range(3):
        grad_hidden = grad_hidden + jnp.dot(grad_pad[(2 - offset) * frame_len:(2 - offset) * frame_len + tokens_all], w_temporal[offset].T, preferred_element_type=jnp.float32)
    grad_pre = (grad_hidden * silu_slope(pre_act)).astype(jnp.bfloat16)
    grad_ws = jnp.stack([jnp.dot(taps[offset].T, grad_pre, preferred_element_type=jnp.float32) for offset in range(9)])
    return grad_ws, grad_wt, grad_wq, grad_wk, grad_wv, grad_wo


def reference(clip, block_ids, w_spatial, w_temporal, w_query, w_key, w_value, w_out, cotangent):
    totals = None
    for which_clip in range(CLIPS):
        grads = one_clip(clip[which_clip], block_ids[which_clip], cotangent[which_clip], w_spatial, w_temporal, w_query, w_key, w_value, w_out)
        if totals is None:
            totals = grads
        else:
            totals = tuple(left + right for left, right in zip(totals, grads))
    factor = (CLIPS * TOKENS) ** -0.5
    return (totals[0] * factor, totals[1] * factor, totals[2] * factor, totals[3] * factor, totals[4] * factor, totals[5] * factor)
```

```python
import jax
import jax.numpy as jnp
from jax import lax
from jax.sharding import Mesh, PartitionSpec as P

HD = 128
SIDE = 8
FRAME = SIDE * SIDE
NEG_FILL = -1e30
BF = jnp.bfloat16
F32 = jnp.float32


def dot(left, right):
    return jnp.dot(left, right, preferred_element_type=F32)


def contract_rows(left, right):
    return lax.dot_general(left, right, (((0,), (0,)), ((), ())), preferred_element_type=F32)


def dot_t(left, right):
    return lax.dot_general(left, right, (((1,), (1,)), ((), ())), preferred_element_type=F32)


def xor_perm(count, step):
    return [(i, i ^ step) for i in range(count)]


def unxor(parts, index):
    parts = list(parts)
    bit = 1
    while bit < len(parts):
        odd = (index & bit) != 0
        parts = [jnp.where(odd, parts[s ^ bit], parts[s]) for s in range(len(parts))]
        bit *= 2
    return parts


def gather_xor(block, axis, count, index):
    parts = [block] + [lax.ppermute(block, axis, xor_perm(count, s)) for s in range(1, count)]
    return unxor(parts, index)


def scatter_xor(total, axis, count, index):
    rows = total.shape[0] // count
    low = total.astype(BF)
    got = [
        lax.ppermute(
            lax.dynamic_slice_in_dim(low, (index ^ s) * rows, rows), axis, xor_perm(count, s)
        )
        for s in range(1, count)
    ]
    own = lax.dynamic_slice_in_dim(total, index * rows, rows)
    for part in got:
        own = own + part.astype(F32)
    return own


def spread(block, axis, count):
    return lax.all_to_all(
        jnp.broadcast_to(block[None], (count,) + block.shape), axis, 0, 0
    )


def shift_rows(field, step):
    if step == 0:
        return field
    pad = jnp.zeros_like(field[:, :1])
    if step > 0:
        return jnp.concatenate([field[:, 1:], pad], axis=1)
    return jnp.concatenate([pad, field[:, :-1]], axis=1)


def shift_cols(field, step):
    if step == 0:
        return field
    pad = jnp.zeros_like(field[:, :, :1])
    if step > 0:
        return jnp.concatenate([field[:, :, 1:], pad], axis=2)
    return jnp.concatenate([pad, field[:, :, :-1]], axis=2)


def shift_frames(tokens, step):
    if step == 0:
        return tokens
    pad = jnp.zeros_like(tokens[:FRAME])
    if step > 0:
        return jnp.concatenate([tokens[FRAME:], pad], axis=0)
    return jnp.concatenate([pad, tokens[:-FRAME]], axis=0)


def on_device(sizes, clip, block_ids, w_spatial, w_temporal, w_query, w_key, w_value, w_out, cotangent):
    n_xh, n_z, n_y, n_c, n_dp = sizes
    i_xh, i_y, i_c, i_dp = (lax.axis_index(a) for a in ("xh", "y", "c", "dp"))
    i_x = i_xh * n_dp + i_dp
    n_head = n_y * n_c
    n_frame = n_xh * n_z
    own_clip = clip[0]
    upstream = cotangent[0]
    ids = block_ids[0]
    local, ch = own_clip.shape
    tokens = local * n_frame
    frames = tokens // FRAME
    scale = HD ** (-0.5)

    piece = local // n_head
    mine = lax.dynamic_slice_in_dim(own_clip, lax.axis_index(("y", "c")) * piece, piece)
    part = spread(mine, "z", n_z)
    part = jnp.stack(gather_xor(part, "xh", n_xh, i_xh))
    part = jnp.stack(gather_xor(part, "y", n_y, i_y))
    part = jnp.stack(gather_xor(part, "c", n_c, i_c))
    whole = part.transpose(2, 3, 1, 0, 4, 5).reshape(frames, SIDE, SIDE, ch)

    cols = jnp.concatenate([shift_cols(whole, b - 1) for b in range(3)], axis=3)
    cols = cols.reshape(tokens, 3 * ch)
    w_sp = w_spatial.reshape(3, 3 * ch, ch).transpose(1, 0, 2).reshape(3 * ch, 3 * ch)
    mixed = dot(cols, w_sp).reshape(frames, SIDE, SIDE, 3 * ch)
    pre = sum(shift_rows(mixed[..., a * ch : (a + 1) * ch], a - 1) for a in range(3))
    pre = pre.reshape(tokens, ch)
    sigma = jax.nn.sigmoid(pre)
    slope = sigma * (1.0 + pre * (1.0 - sigma))
    hidden = (pre * sigma).astype(BF)
    around = jnp.concatenate([shift_frames(hidden, d - 1) for d in range(3)], axis=1)
    features = dot(around, w_temporal.reshape(3 * ch, ch)).astype(BF)

    keys = dot(features, w_key).astype(BF)
    values = dot(features, w_value).astype(BF)
    first = lax.axis_index(("xh", "z")) * local
    own_feat = lax.dynamic_slice_in_dim(features, first, local)
    queries = dot(own_feat, w_query).astype(BF)
    grad_att = dot_t(upstream, w_out).astype(BF)
    visible = ids[None, :] <= lax.dynamic_slice_in_dim(ids, first, local)[:, None]
    att_parts, gq_parts, gk_parts, gv_parts = [], [], [], []
    for h in range(queries.shape[1] // HD):
        sel = slice(h * HD, (h + 1) * HD)
        q_h, k_h, v_h, g_h = queries[:, sel], keys[:, sel], values[:, sel], grad_att[:, sel]
        scores = jnp.where(visible, dot_t(q_h, k_h) * scale, NEG_FILL)
        top = jnp.max(scores, axis=1, keepdims=True)
        total = jnp.sum(jnp.where(visible, jnp.exp(scores - top), 0.0), axis=1, keepdims=True)
        log_norm = top + jnp.log(total)
        probs = jnp.where(visible, jnp.exp(scores - log_norm), 0.0)
        probs_low = probs.astype(BF)
        att = dot(probs_low, v_h).astype(BF)
        delta = jnp.sum(g_h.astype(F32) * att.astype(F32), axis=1, keepdims=True)
        grad_scores = (probs * (dot_t(g_h, v_h) - delta) * scale).astype(BF)
        att_parts.append(att)
        gq_parts.append(dot(grad_scores, k_h).astype(BF))
        gk_parts.append(contract_rows(grad_scores, q_h).astype(BF))
        gv_parts.append(contract_rows(probs_low, g_h).astype(BF))
    att = jnp.concatenate(att_parts, axis=1)
    gq = jnp.concatenate(gq_parts, axis=1)
    gk = jnp.concatenate(gk_parts, axis=1)
    gv = jnp.concatenate(gv_parts, axis=1)

    gf = dot_t(gk, w_key) + dot_t(gv, w_value)
    own_gf = dot_t(gq, w_query) + upstream.astype(F32) * (1.0 / n_head)
    own_gf = own_gf + lax.dynamic_slice_in_dim(gf, first, local)
    gf = lax.dynamic_update_slice_in_dim(gf, own_gf, first, 0).astype(BF)
    g_wt = contract_rows(around, gf)
    back = jnp.concatenate([shift_frames(gf, 1 - d) for d in range(3)], axis=1)
    w_tt = w_temporal.transpose(0, 2, 1).reshape(3 * ch, ch)
    grad_pre = dot(back, w_tt) * slope
    grad_pre = grad_pre.reshape(frames, SIDE, SIDE, ch)
    rows = jnp.concatenate([shift_rows(grad_pre, 1 - a).astype(BF) for a in range(3)], axis=3)
    g_ws = contract_rows(cols, rows.reshape(tokens, 3 * ch))
    g_ws = g_ws.reshape(3, ch, 3, ch).transpose(2, 0, 1, 3).reshape(9 * ch, ch)
    g_head = jnp.concatenate(
        [
            contract_rows(own_feat, gq),
            contract_rows(features, gk),
            contract_rows(features, gv),
            contract_rows(att, upstream),
        ]
    )

    shared = jnp.concatenate([g_ws, g_wt])
    shared = scatter_xor(shared, "c", n_c, i_c)
    shared = scatter_xor(shared, "y", n_y, i_y)
    block = jnp.concatenate([shared, g_head])
    n_x = n_xh * n_dp
    block = scatter_xor(block, ("xh", "dp"), n_x, i_x)
    rows = block.shape[0] // n_z
    got = lax.all_to_all(block.astype(BF).reshape(n_z, rows, ch), "z", 0, 0)
    factor = float(n_dp * tokens) ** (-0.5)
    done = (jnp.sum(got.astype(F32), axis=0) * factor).astype(BF)
    done = spread(done, "z", n_z).reshape(n_z * rows, ch)
    done = jnp.concatenate(gather_xor(done, ("xh", "dp"), n_x, i_x))
    cut = shared.shape[0]
    heads = done[cut:].astype(F32).reshape(4, ch, -1)
    done = jnp.concatenate(gather_xor(done[:cut], "y", n_y, i_y))
    done = jnp.concatenate(gather_xor(done, "c", n_c, i_c)).astype(F32)
    return (
        done[: 9 * ch].reshape(9, ch, ch),
        done[9 * ch :].reshape(3, ch, ch),
        heads[0],
        heads[1],
        heads[2],
        heads[3],
    )


def solution(mesh):
    frame, head, dp = (mesh.shape[a] for a in ("frame", "head", "dp"))
    sizes = (2, frame // 2, head // 2, 2, dp)
    names = ("xh", "z", "y", "c", "dp")
    fine = Mesh(mesh.devices.reshape(sizes), names)
    rows, head_axes = ("xh", "z"), ("y", "c")
    in_specs = (
        P("dp", rows, None),
        P("dp", None),
        P(),
        P(),
        P(None, head_axes),
        P(None, head_axes),
        P(None, head_axes),
        P(head_axes, None),
        P("dp", rows, None),
    )
    out_specs = (
        P(),
        P(),
        P(None, head_axes),
        P(None, head_axes),
        P(None, head_axes),
        P(head_axes, None),
    )

    def body(*args):
        return on_device(sizes, *args)

    return jax.shard_map(
        body, mesh=fine, in_specs=in_specs, out_specs=out_specs, check_vma=False
    )
```

```python
import functools

import jax
import jax.numpy as jnp
from jax import lax
from jax.experimental import pallas as pl
from jax.experimental.pallas import tpu as pltpu
from jax.sharding import Mesh, PartitionSpec as P

HD = 128
SIDE = 8
FRAME = SIDE * SIDE
NEG_FILL = -1e30
LOG2E = 1.4426950408889634
BF = jnp.bfloat16
F32 = jnp.float32


def dot(left, right):
    return jnp.dot(left, right, preferred_element_type=F32)


def contract_rows(left, right):
    return lax.dot_general(left, right, (((0,), (0,)), ((), ())), preferred_element_type=F32)


def dot_t(left, right):
    return lax.dot_general(left, right, (((1,), (1,)), ((), ())), preferred_element_type=F32)


def xor_perm(count, step):
    return [(i, i ^ step) for i in range(count)]


def unxor(parts, index):
    parts = list(parts)
    bit = 1
    while bit < len(parts):
        odd = (index & bit) != 0
        parts = [jnp.where(odd, parts[s ^ bit], parts[s]) for s in range(len(parts))]
        bit *= 2
    return parts


def gather_xor(block, axis, count, index):
    parts = [block] + [lax.ppermute(block, axis, xor_perm(count, s)) for s in range(1, count)]
    return unxor(parts, index)


def scatter_xor(total, axis, count, index):
    rows = total.shape[0] // count
    low = total.astype(BF)
    got = [
        lax.ppermute(
            lax.dynamic_slice_in_dim(low, (index ^ s) * rows, rows), axis, xor_perm(count, s)
        )
        for s in range(1, count)
    ]
    own = lax.dynamic_slice_in_dim(total, index * rows, rows)
    for part in got:
        own = own + part.astype(F32)
    return own


def spread(block, axis, count):
    return lax.all_to_all(
        jnp.broadcast_to(block[None], (count,) + block.shape), axis, 0, 0
    )


def roll_cols(block, step):
    groups = block.reshape(-1, SIDE, block.shape[1])
    place = lax.broadcasted_iota(jnp.int32, groups.shape, 1)
    if step < 0:
        moved = jnp.where(place == 0, 0.0, pltpu.roll(groups, 1, 1))
    else:
        moved = jnp.where(place == SIDE - 1, 0.0, pltpu.roll(groups, SIDE - 1, 1))
    return moved.reshape(block.shape)


def move_rows(field, step):
    pad = jnp.zeros((field.shape[0], SIDE, field.shape[2]), field.dtype)
    if step > 0:
        return jnp.concatenate([field[:, SIDE:], pad], axis=1)
    return jnp.concatenate([pad, field[:, :-SIDE]], axis=1)


def local_kernel(
    dims,
    pos,
    ids_ref,
    own_ids_ref,
    *refs,
):
    n_xh, n_z, n_y, n_c, chunk = dims
    n_parts = n_y * n_c
    parts = refs[:n_parts]
    w_sp, w_t, w_q, w_k, w_v, w_o, up_ref = refs[n_parts : n_parts + 7]
    send_ref, keep_ref, head_ref = refs[n_parts + 7 : n_parts + 10]
    (
        cols,
        slope,
        hid,
        feat,
        keys,
        values,
        gkey,
        gval,
        gf,
        e_ref,
        acc,
        q_ref,
        g_ref,
        att_ref,
        gq_ref,
    ) = refs[n_parts + 10 :]
    my_xh, my_y, my_c = pos[0], pos[1], pos[2]
    first = pl.multiple_of(pos[3], 256)
    tokens, ch = feat.shape
    local = up_ref.shape[0]
    half = parts[0].shape[2]
    n_chunk = tokens // chunk
    frames = chunk // FRAME
    scale = HD ** (-0.5)
    n_head = n_y * n_c

    @pl.loop(0, n_z)
    def _(z):
        for s in range(n_y):
            for t in range(n_c):
                for u in range(n_xh):
                    frame = ((my_xh ^ u) * n_z + z) * n_y + (my_y ^ s)
                    row = pl.multiple_of(frame * FRAME + (my_c ^ t) * half, half)
                    low = parts[s * n_c + t][u, z]
                    wide = low.astype(F32)
                    cols[pl.ds(row, half), 0:ch] = roll_cols(wide, -1).astype(BF)
                    cols[pl.ds(row, half), ch : 2 * ch] = low
                    cols[pl.ds(row, half), 2 * ch : 3 * ch] = roll_cols(wide, 1).astype(BF)

    edge = jnp.zeros((FRAME, ch), BF)
    hid[0:FRAME, :] = edge
    hid[tokens + FRAME : tokens + 2 * FRAME, :] = edge
    gf[0:FRAME, :] = edge
    gf[tokens + FRAME : tokens + 2 * FRAME, :] = edge
    acc[...] = jnp.zeros_like(acc)
    head_ref[...] = jnp.zeros_like(head_ref)

    @pl.loop(0, n_chunk)
    def _(i):
        row = pl.multiple_of(i * chunk, chunk)
        x = cols[pl.ds(row, chunk), :]
        mix = [
            dot(x, w_sp[a * 3 * ch : (a + 1) * 3 * ch, :]).reshape(frames, FRAME, ch)
            for a in range(3)
        ]
        pre = mix[1] + move_rows(mix[0], -1) + move_rows(mix[2], 1)
        pre = pre.reshape(chunk, ch)
        sigma = jax.nn.sigmoid(pre)
        slope[pl.ds(row, chunk), :] = sigma * (1.0 + pre * (1.0 - sigma))
        hid[pl.ds(pl.multiple_of(row + FRAME, FRAME), chunk), :] = (pre * sigma).astype(BF)

    @pl.loop(0, n_chunk)
    def _(i):
        row = pl.multiple_of(i * chunk, chunk)
        total = dot(hid[pl.ds(row, chunk), :], w_t[0:ch, :])
        for d in range(1, 3):
            at = pl.multiple_of(row + d * FRAME, FRAME)
            total = total + dot(hid[pl.ds(at, chunk), :], w_t[d * ch : (d + 1) * ch, :])
        low = total.astype(BF)
        feat[pl.ds(row, chunk), :] = low
        keys[pl.ds(row, chunk), :] = dot(low, w_k[...]).astype(BF)
        values[pl.ds(row, chunk), :] = dot(low, w_v[...]).astype(BF)

    q_ref[...] = dot(feat[pl.ds(first, local), :], w_q[...]).astype(BF)
    g_ref[...] = dot_t(up_ref[...], w_o[...]).astype(BF)

    def fold(block, join):
        out = block[:, 0:HD]
        for k in range(1, block.shape[1] // HD):
            out = join(out, block[:, k * HD : (k + 1) * HD])
        return out

    for h in range(q_ref.shape[1] // HD):
        sel = slice(h * HD, (h + 1) * HD)

        def raw(i, top):
            row = pl.multiple_of(i * chunk, chunk)
            s = dot_t(q_ref[:, sel], keys[pl.ds(row, chunk), sel])
            s = jnp.where(ids_ref[:, pl.ds(row, chunk)] <= own_ids_ref[...], s, NEG_FILL)
            e_ref[:, pl.ds(row, chunk)] = s
            return jnp.maximum(top, fold(s, jnp.maximum))

        top = lax.fori_loop(0, n_chunk, raw, jnp.full((local, HD), NEG_FILL, F32))
        top = jnp.max(top, axis=1, keepdims=True)

        def forward(i, carry):
            total, out = carry
            row = pl.multiple_of(i * chunk, chunk)
            e = jnp.exp2((e_ref[:, pl.ds(row, chunk)] - top) * (scale * LOG2E))
            e_ref[:, pl.ds(row, chunk)] = e
            total = total + fold(e, jnp.add)
            return total, out + dot(e.astype(BF), values[pl.ds(row, chunk), sel])

        zero = jnp.zeros((local, HD), F32)
        total, out = lax.fori_loop(0, n_chunk, forward, (zero, zero))
        inv = 1.0 / jnp.sum(total, axis=1, keepdims=True)
        att = (out * inv).astype(BF)
        att_ref[:, sel] = att
        delta = jnp.sum(g_ref[:, sel].astype(F32) * att.astype(F32), axis=1, keepdims=True)

        def backward(i, gq):
            row = pl.multiple_of(i * chunk, chunk)
            p = e_ref[:, pl.ds(row, chunk)] * inv
            g = g_ref[:, sel]
            k = keys[pl.ds(row, chunk), sel]
            ds = (p * (dot_t(g, values[pl.ds(row, chunk), sel]) - delta)).astype(BF)
            gkey[pl.ds(row, chunk), sel] = (contract_rows(ds, q_ref[:, sel]) * scale).astype(BF)
            gval[pl.ds(row, chunk), sel] = contract_rows(p.astype(BF), g).astype(BF)
            return gq + dot(ds, k)

        gq = lax.fori_loop(0, n_chunk, backward, zero)
        gq_ref[:, sel] = (gq * scale).astype(BF)

    @pl.loop(0, n_chunk)
    def _(i):
        row = pl.multiple_of(i * chunk, chunk)
        gk, gv = gkey[pl.ds(row, chunk), :], gval[pl.ds(row, chunk), :]
        f = feat[pl.ds(row, chunk), :]
        at = pl.multiple_of(row + FRAME, FRAME)
        gf[pl.ds(at, chunk), :] = (dot_t(gk, w_k[...]) + dot_t(gv, w_v[...])).astype(BF)
        head_ref[ch : 2 * ch, :] += contract_rows(f, gk)
        head_ref[2 * ch : 3 * ch, :] += contract_rows(f, gv)

    own = pl.ds(first, local)
    up = up_ref[...]
    total = dot_t(gkey[own, :], w_k[...]) + dot_t(gval[own, :], w_v[...])
    total = total + dot_t(gq_ref[...], w_q[...]) + up.astype(F32) * (1.0 / n_head)
    gf[pl.ds(pl.multiple_of(first + FRAME, FRAME), local), :] = total.astype(BF)
    head_ref[0:ch, :] = contract_rows(feat[own, :], gq_ref[...])
    head_ref[3 * ch : 4 * ch, :] = contract_rows(att_ref[...], up)

    @pl.loop(0, n_chunk)
    def _(i):
        row = pl.multiple_of(i * chunk, chunk)
        here = gf[pl.ds(pl.multiple_of(row + FRAME, FRAME), chunk), :]
        back = jnp.zeros((chunk, ch), F32)
        for d in range(3):
            at = pl.multiple_of(row + d * FRAME, FRAME)
            acc[(9 + d) * ch : (10 + d) * ch, :] += contract_rows(hid[pl.ds(at, chunk), :], here)
            at = pl.multiple_of(row + (2 - d) * FRAME, FRAME)
            back = back + dot_t(gf[pl.ds(at, chunk), :], w_t[d * ch : (d + 1) * ch, :])
        gp = (back * slope[pl.ds(row, chunk), :]).reshape(frames, FRAME, ch)
        x = cols[pl.ds(row, chunk), :]
        for a in range(3):
            moved = gp if a == 1 else move_rows(gp, 1 - a)
            moved = moved.reshape(chunk, ch).astype(BF)
            acc[a * 3 * ch : (a + 1) * 3 * ch, :] += contract_rows(x, moved)

    half_rows = keep_ref.shape[0]
    send_ref[...] = acc[pl.ds(pl.multiple_of((1 - my_c) * half_rows, half_rows), half_rows), :].astype(BF)
    keep_ref[...] = acc[pl.ds(pl.multiple_of(my_c * half_rows, half_rows), half_rows), :]


def local_terms(sizes, pos, ids, own_ids, parts, weights, up, chunk=512):
    n_xh, n_z, n_y, n_c, _ = sizes
    local, ch = up.shape
    tokens = local * n_xh * n_z
    wide = weights[2].shape[1]
    dims = (n_xh, n_z, n_y, n_c, chunk)
    vm = pl.BlockSpec(memory_space=pltpu.VMEM)
    n_in = 2 + len(parts) + len(weights) + 1
    return pl.pallas_call(
        functools.partial(local_kernel, dims),
        name="local_terms",
        out_shape=(
            jax.ShapeDtypeStruct((6 * ch, ch), BF),
            jax.ShapeDtypeStruct((6 * ch, ch), F32),
            jax.ShapeDtypeStruct((4 * ch, ch), F32),
        ),
        in_specs=[pl.BlockSpec(memory_space=pltpu.SMEM)] + [vm] * n_in,
        out_specs=(vm, vm, vm),
        scratch_shapes=[
            pltpu.VMEM((tokens, 3 * ch), BF),
            pltpu.VMEM((tokens, ch), F32),
            pltpu.VMEM((tokens + 2 * FRAME, ch), BF),
            pltpu.VMEM((tokens, ch), BF),
            pltpu.VMEM((tokens, wide), BF),
            pltpu.VMEM((tokens, wide), BF),
            pltpu.VMEM((tokens, wide), BF),
            pltpu.VMEM((tokens, wide), BF),
            pltpu.VMEM((tokens + 2 * FRAME, ch), BF),
            pltpu.VMEM((local, tokens), F32),
            pltpu.VMEM((12 * ch, ch), F32),
            pltpu.VMEM((local, wide), BF),
            pltpu.VMEM((local, wide), BF),
            pltpu.VMEM((local, wide), BF),
            pltpu.VMEM((local, wide), BF),
        ],
        compiler_params=pltpu.CompilerParams(vmem_limit_bytes=58 * 2**20),
        cost_estimate=pl.CostEstimate(
            flops=24 * 10**9, transcendentals=2 * local * tokens, bytes_accessed=12 * 2**20
        ),
    )(pos, ids, own_ids, *parts, *weights, up)


def on_device(sizes, clip, block_ids, w_spatial, w_temporal, w_query, w_key, w_value, w_out, cotangent):
    n_xh, n_z, n_y, n_c, n_dp = sizes
    i_xh, i_y, i_c, i_dp = (lax.axis_index(a) for a in ("xh", "y", "c", "dp"))
    i_x = i_xh * n_dp + i_dp
    n_head = n_y * n_c
    n_frame = n_xh * n_z
    own_clip = clip[0]
    upstream = cotangent[0]
    ids = block_ids[0]
    local, ch = own_clip.shape
    tokens = local * n_frame

    piece = local // n_head
    mine = lax.dynamic_slice_in_dim(own_clip, lax.axis_index(("y", "c")) * piece, piece)
    part = spread(mine, "z", n_z)
    part = jnp.stack([part, lax.ppermute(part, "xh", xor_perm(n_xh, 1))])
    parts = []
    for s in range(n_y):
        block = part if s == 0 else lax.ppermute(part, "y", xor_perm(n_y, s))
        parts += [block, lax.ppermute(block, "c", xor_perm(n_c, 1))]

    first = lax.axis_index(("xh", "z")) * local
    pos = jnp.stack([i_xh, i_y, i_c, first]).astype(jnp.int32)
    own_ids = lax.dynamic_slice_in_dim(ids, first, local)[:, None]
    weights = (
        w_spatial.reshape(9 * ch, ch),
        w_temporal.reshape(3 * ch, ch),
        w_query,
        w_key,
        w_value,
        w_out,
    )
    send, keep, g_head = local_terms(sizes, pos, ids[None], own_ids, parts, weights, upstream)

    shared = keep + lax.ppermute(send, "c", xor_perm(n_c, 1)).astype(F32)
    shared = scatter_xor(shared, "y", n_y, i_y)
    block = jnp.concatenate([shared, g_head])
    n_x = n_xh * n_dp
    block = scatter_xor(block, ("xh", "dp"), n_x, i_x)
    rows = block.shape[0] // n_z
    got = lax.all_to_all(block.astype(BF).reshape(n_z, rows, ch), "z", 0, 0)
    factor = float(n_dp * tokens) ** (-0.5)
    done = (jnp.sum(got.astype(F32), axis=0) * factor).astype(BF)
    done = spread(done, "z", n_z).reshape(n_z * rows, ch)
    done = jnp.concatenate(gather_xor(done, ("xh", "dp"), n_x, i_x))
    cut = shared.shape[0]
    heads = done[cut:].astype(F32).reshape(4, ch, -1)
    done = jnp.concatenate(gather_xor(done[:cut], "y", n_y, i_y))
    done = jnp.concatenate(gather_xor(done, "c", n_c, i_c)).astype(F32)
    return (
        done[: 9 * ch].reshape(9, ch, ch),
        done[9 * ch :].reshape(3, ch, ch),
        heads[0],
        heads[1],
        heads[2],
        heads[3],
    )


def solution(mesh):
    frame, head, dp = (mesh.shape[a] for a in ("frame", "head", "dp"))
    sizes = (2, frame // 2, head // 2, 2, dp)
    names = ("xh", "z", "y", "c", "dp")
    fine = Mesh(mesh.devices.reshape(sizes), names)
    rows, head_axes = ("xh", "z"), ("y", "c")
    in_specs = (
        P("dp", rows, None),
        P("dp", None),
        P(),
        P(),
        P(None, head_axes),
        P(None, head_axes),
        P(None, head_axes),
        P(head_axes, None),
        P("dp", rows, None),
    )
    out_specs = (
        P(),
        P(),
        P(None, head_axes),
        P(None, head_axes),
        P(None, head_axes),
        P(head_axes, None),
    )

    def body(*args):
        return on_device(sizes, *args)

    return jax.shard_map(
        body, mesh=fine, in_specs=in_specs, out_specs=out_specs, check_vma=False
    )
```

```python
import functools

import jax
import jax.numpy as jnp
from jax import lax
from jax.experimental import pallas as pl
from jax.experimental.pallas import tpu as pltpu
from jax.sharding import Mesh, PartitionSpec as P

HD = 128
SIDE = 8
FRAME = SIDE * SIDE
NEG_FILL = -1e30
LOG2E = 1.4426950408889634
BF = jnp.bfloat16
F32 = jnp.float32


def dot(left, right):
    return jnp.dot(left, right, preferred_element_type=F32)


def contract_rows(left, right):
    return lax.dot_general(left, right, (((0,), (0,)), ((), ())), preferred_element_type=F32)


def dot_t(left, right):
    return lax.dot_general(left, right, (((1,), (1,)), ((), ())), preferred_element_type=F32)


def xor_perm(count, step):
    return [(i, i ^ step) for i in range(count)]


def unxor(parts, index):
    parts = list(parts)
    bit = 1
    while bit < len(parts):
        odd = (index & bit) != 0
        parts = [jnp.where(odd, parts[s ^ bit], parts[s]) for s in range(len(parts))]
        bit *= 2
    return parts


def gather_xor(block, axis, count, index):
    parts = [block] + [lax.ppermute(block, axis, xor_perm(count, s)) for s in range(1, count)]
    return unxor(parts, index)


def spread(block, axis, count):
    return lax.all_to_all(
        jnp.broadcast_to(block[None], (count,) + block.shape), axis, 0, 0
    )


def roll_cols(block, step):
    groups = block.reshape(-1, SIDE, block.shape[1])
    place = lax.broadcasted_iota(jnp.int32, groups.shape, 1)
    if step < 0:
        moved = jnp.where(place == 0, 0.0, pltpu.roll(groups, 1, 1))
    else:
        moved = jnp.where(place == SIDE - 1, 0.0, pltpu.roll(groups, SIDE - 1, 1))
    return moved.reshape(block.shape)


def move_rows(field, step):
    pad = jnp.zeros((field.shape[0], SIDE, field.shape[2]), field.dtype)
    if step > 0:
        return jnp.concatenate([field[:, SIDE:], pad], axis=1)
    return jnp.concatenate([pad, field[:, :-SIDE]], axis=1)


def local_kernel(
    dims,
    pos,
    ids_ref,
    *refs,
):
    n_xh, n_z, n_y, n_c, n_dp = dims
    n_x = n_xh * n_dp
    n_parts = n_xh * n_y * n_c
    parts = refs[:n_parts]
    w_sp, w_t, w_q, w_k, w_v, w_o, up_ref = refs[n_parts : n_parts + 7]
    outs = refs[n_parts + 7 : n_parts + 7 + 2 * n_y + n_x]
    send_refs, keep_refs, head_refs = outs[:n_y], outs[n_y : 2 * n_y], outs[2 * n_y :]
    (
        cols,
        slope,
        hid,
        feat,
        keys,
        values,
        gkey,
        gval,
        gf,
        e_ref,
        acc,
        heads,
        q_ref,
        g_ref,
        att_ref,
        gq_ref,
    ) = refs[n_parts + 7 + 2 * n_y + n_x :]
    my_xh, my_y, my_c, my_x = pos[0], pos[1], pos[2], pos[4]
    first = pl.multiple_of(pos[3], up_ref.shape[0])
    tokens, ch = feat.shape
    local = up_ref.shape[0]
    half = parts[0].shape[1]
    scale = HD ** (-0.5)
    n_head = n_y * n_c
    own_ids = jnp.broadcast_to(ids_ref[:, pl.ds(first, local)].astype(F32), (SIDE, local))
    own_ids = jnp.transpose(own_ids)[:, 0:1].astype(jnp.int32)

    @pl.loop(0, n_z)
    def _(z):
        for u in range(n_xh):
            for s in range(n_y):
                for t in range(n_c):
                    frame = ((my_xh ^ u) * n_z + z) * n_y + (my_y ^ s)
                    row = pl.multiple_of(frame * FRAME + (my_c ^ t) * half, half)
                    low = parts[(u * n_y + s) * n_c + t][z]
                    wide = low.astype(F32)
                    cols[pl.ds(row, half), 0:ch] = roll_cols(wide, -1).astype(BF)
                    cols[pl.ds(row, half), ch : 2 * ch] = low
                    cols[pl.ds(row, half), 2 * ch : 3 * ch] = roll_cols(wide, 1).astype(BF)

    edge = jnp.zeros((FRAME, ch), BF)
    hid[0:FRAME, :] = edge
    hid[tokens + FRAME : tokens + 2 * FRAME, :] = edge
    gf[0:FRAME, :] = edge
    gf[tokens + FRAME : tokens + 2 * FRAME, :] = edge
    acc[...] = jnp.zeros_like(acc)
    heads[...] = jnp.zeros_like(heads)

    chunk = min(tokens, 1024)
    n_chunk = tokens // chunk
    frames = chunk // FRAME
    @pl.loop(0, n_chunk)
    def _(i):
        row = pl.multiple_of(i * chunk, chunk)
        x = cols[pl.ds(row, chunk), :]
        mix = [
            dot(x, w_sp[a * 3 * ch : (a + 1) * 3 * ch, :]).reshape(frames, FRAME, ch)
            for a in range(3)
        ]
        pre = mix[1] + move_rows(mix[0], -1) + move_rows(mix[2], 1)
        pre = pre.reshape(chunk, ch)
        sigma = jax.nn.sigmoid(pre)
        slope[pl.ds(row, chunk), :] = sigma * (1.0 + pre * (1.0 - sigma))
        hid[pl.ds(pl.multiple_of(row + FRAME, FRAME), chunk), :] = (pre * sigma).astype(BF)

    chunk = min(tokens, 1024)
    n_chunk = tokens // chunk
    @pl.loop(0, n_chunk)
    def _(i):
        row = pl.multiple_of(i * chunk, chunk)
        total = dot(hid[pl.ds(row, chunk), :], w_t[0:ch, :])
        for d in range(1, 3):
            at = pl.multiple_of(row + d * FRAME, FRAME)
            total = total + dot(hid[pl.ds(at, chunk), :], w_t[d * ch : (d + 1) * ch, :])
        low = total.astype(BF)
        feat[pl.ds(row, chunk), :] = low
        keys[pl.ds(row, chunk), :] = dot(low, w_k[...]).astype(BF)
        values[pl.ds(row, chunk), :] = dot(low, w_v[...]).astype(BF)

    q_ref[...] = dot(feat[pl.ds(first, local), :], w_q[...]).astype(BF)
    g_ref[...] = dot_t(up_ref[...], w_o[...]).astype(BF)

    chunk = min(tokens, 2048)
    n_chunk = tokens // chunk
    def fold(block, join):
        out = block[:, 0:HD]
        for k in range(1, block.shape[1] // HD):
            out = join(out, block[:, k * HD : (k + 1) * HD])
        return out

    for h in range(q_ref.shape[1] // HD):
        sel = slice(h * HD, (h + 1) * HD)

        def raw(i, top):
            row = pl.multiple_of(i * chunk, chunk)
            s = dot_t(q_ref[:, sel], keys[pl.ds(row, chunk), sel])
            s = jnp.where(ids_ref[:, pl.ds(row, chunk)] <= own_ids, s, NEG_FILL)
            e_ref[:, pl.ds(row, chunk)] = s
            return jnp.maximum(top, fold(s, jnp.maximum))

        top = lax.fori_loop(0, n_chunk, raw, jnp.full((local, HD), NEG_FILL, F32))
        top = jnp.max(top, axis=1, keepdims=True)

        def forward(i, carry):
            total, out = carry
            row = pl.multiple_of(i * chunk, chunk)
            e = jnp.exp2((e_ref[:, pl.ds(row, chunk)] - top) * (scale * LOG2E))
            e_ref[:, pl.ds(row, chunk)] = e
            total = total + fold(e, jnp.add)
            return total, out + dot(e.astype(BF), values[pl.ds(row, chunk), sel])

        zero = jnp.zeros((local, HD), F32)
        total, out = lax.fori_loop(0, n_chunk, forward, (zero, zero))
        inv = 1.0 / jnp.sum(total, axis=1, keepdims=True)
        att = (out * inv).astype(BF)
        att_ref[:, sel] = att
        delta = jnp.sum(g_ref[:, sel].astype(F32) * att.astype(F32), axis=1, keepdims=True)

        def backward(i, gq):
            row = pl.multiple_of(i * chunk, chunk)
            p = e_ref[:, pl.ds(row, chunk)] * inv
            g = g_ref[:, sel]
            k = keys[pl.ds(row, chunk), sel]
            ds = (p * (dot_t(g, values[pl.ds(row, chunk), sel]) - delta)).astype(BF)
            gkey[pl.ds(row, chunk), sel] = (contract_rows(ds, q_ref[:, sel]) * scale).astype(BF)
            gval[pl.ds(row, chunk), sel] = contract_rows(p.astype(BF), g).astype(BF)
            return gq + dot(ds, k)

        gq = lax.fori_loop(0, n_chunk, backward, zero)
        gq_ref[:, sel] = (gq * scale).astype(BF)

    chunk = min(tokens, 1024)
    n_chunk = tokens // chunk
    @pl.loop(0, n_chunk)
    def _(i):
        row = pl.multiple_of(i * chunk, chunk)
        gk, gv = gkey[pl.ds(row, chunk), :], gval[pl.ds(row, chunk), :]
        f = feat[pl.ds(row, chunk), :]
        at = pl.multiple_of(row + FRAME, FRAME)
        gf[pl.ds(at, chunk), :] = (dot_t(gk, w_k[...]) + dot_t(gv, w_v[...])).astype(BF)
        heads[ch : 2 * ch, :] += contract_rows(f, gk)
        heads[2 * ch : 3 * ch, :] += contract_rows(f, gv)

    own = pl.ds(first, local)
    up = up_ref[...]
    total = dot_t(gkey[own, :], w_k[...]) + dot_t(gval[own, :], w_v[...])
    total = total + dot_t(gq_ref[...], w_q[...]) + up.astype(F32) * (1.0 / n_head)
    gf[pl.ds(pl.multiple_of(first + FRAME, FRAME), local), :] = total.astype(BF)
    heads[0:ch, :] = contract_rows(feat[own, :], gq_ref[...])
    heads[3 * ch : 4 * ch, :] = contract_rows(att_ref[...], up)

    chunk = min(tokens, 1024)
    n_chunk = tokens // chunk
    frames = chunk // FRAME
    @pl.loop(0, n_chunk)
    def _(i):
        row = pl.multiple_of(i * chunk, chunk)
        here = gf[pl.ds(pl.multiple_of(row + FRAME, FRAME), chunk), :]
        back = jnp.zeros((chunk, ch), F32)
        for d in range(3):
            at = pl.multiple_of(row + d * FRAME, FRAME)
            acc[(9 + d) * ch : (10 + d) * ch, :] += contract_rows(hid[pl.ds(at, chunk), :], here)
            at = pl.multiple_of(row + (2 - d) * FRAME, FRAME)
            back = back + dot_t(gf[pl.ds(at, chunk), :], w_t[d * ch : (d + 1) * ch, :])
        gp = (back * slope[pl.ds(row, chunk), :]).reshape(frames, FRAME, ch)
        x = cols[pl.ds(row, chunk), :]
        for a in range(3):
            moved = gp if a == 1 else move_rows(gp, 1 - a)
            moved = moved.reshape(chunk, ch).astype(BF)
            acc[a * 3 * ch : (a + 1) * 3 * ch, :] += contract_rows(x, moved)

    rows = keep_refs[0].shape[0]
    sub = rows // n_x
    for s in range(n_y):
        for r in range(n_x):
            at = (my_y ^ s) * rows + (my_x ^ r) * sub
            here = slice(r * sub, (r + 1) * sub)
            for ref, which in ((send_refs[s], 1 - my_c), (keep_refs[s], my_c)):
                row = pl.multiple_of(which * (n_y * rows) + at, SIDE)
                ref[here, :] = acc[pl.ds(row, sub), :].astype(BF)
    for r in range(n_x):
        head_refs[r][...] = heads[pl.ds(pl.multiple_of((my_x ^ r) * ch, ch), ch), :].astype(BF)


def local_terms(sizes, pos, ids, parts, weights, up):
    n_xh, n_z, n_y, n_c, n_dp = sizes
    n_x = n_xh * n_dp
    local, ch = up.shape
    tokens = local * n_xh * n_z
    wide = weights[2].shape[1]
    block = 12 * ch // (n_c * n_y)
    vm = pl.BlockSpec(memory_space=pltpu.VMEM)
    n_in = 1 + len(parts) + len(weights) + 1
    shapes = [(block, ch)] * (2 * n_y) + [(4 * ch // n_x, ch)] * n_x
    out = pl.pallas_call(
        functools.partial(local_kernel, sizes),
        name="local_terms",
        out_shape=[jax.ShapeDtypeStruct(s, BF) for s in shapes],
        in_specs=[pl.BlockSpec(memory_space=pltpu.SMEM)] + [vm] * n_in,
        out_specs=[vm] * len(shapes),
        scratch_shapes=[
            pltpu.VMEM((tokens, 3 * ch), BF),
            pltpu.VMEM((tokens, ch), F32),
            pltpu.VMEM((tokens + 2 * FRAME, ch), BF),
            pltpu.VMEM((tokens, ch), BF),
            pltpu.VMEM((tokens, wide), BF),
            pltpu.VMEM((tokens, wide), BF),
            pltpu.VMEM((tokens, wide), BF),
            pltpu.VMEM((tokens, wide), BF),
            pltpu.VMEM((tokens + 2 * FRAME, ch), BF),
            pltpu.VMEM((local, tokens), F32),
            pltpu.VMEM((12 * ch, ch), F32),
            pltpu.VMEM((4 * ch, ch), F32),
            pltpu.VMEM((local, wide), BF),
            pltpu.VMEM((local, wide), BF),
            pltpu.VMEM((local, wide), BF),
            pltpu.VMEM((local, wide), BF),
        ],
        compiler_params=pltpu.CompilerParams(vmem_limit_bytes=58 * 2**20),
        cost_estimate=pl.CostEstimate(
            flops=24 * 10**9, transcendentals=2 * local * tokens, bytes_accessed=12 * 2**20
        ),
    )(pos, ids, *parts, *weights, up)
    return out[:n_y], out[n_y : 2 * n_y], out[2 * n_y :]


def on_device(sizes, clip, block_ids, w_spatial, w_temporal, w_query, w_key, w_value, w_out, cotangent):
    n_xh, n_z, n_y, n_c, n_dp = sizes
    i_xh, i_y, i_c, i_dp = (lax.axis_index(a) for a in ("xh", "y", "c", "dp"))
    i_x = i_xh * n_dp + i_dp
    n_head = n_y * n_c
    n_frame = n_xh * n_z
    own_clip = clip[0]
    upstream = cotangent[0]
    ids = block_ids[0]
    local, ch = own_clip.shape
    tokens = local * n_frame

    piece = local // n_head
    mine = lax.dynamic_slice_in_dim(own_clip, lax.axis_index(("y", "c")) * piece, piece)
    part = spread(mine, "z", n_z)
    parts = []
    for u in range(n_xh):
        held = part if u == 0 else lax.ppermute(part, "xh", xor_perm(n_xh, u))
        for s in range(n_y):
            block = held if s == 0 else lax.ppermute(held, "y", xor_perm(n_y, s))
            parts += [block, lax.ppermute(block, "c", xor_perm(n_c, 1))]

    first = lax.axis_index(("xh", "z")) * local
    pos = jnp.stack([i_xh, i_y, i_c, first, i_x]).astype(jnp.int32)
    weights = (
        w_spatial.reshape(9 * ch, ch),
        w_temporal.reshape(3 * ch, ch),
        w_query,
        w_key,
        w_value,
        w_out,
    )
    send, keep, heads = local_terms(sizes, pos, ids[None], parts, weights, upstream)

    n_x = n_xh * n_dp
    x_axes = ("xh", "dp")
    other = [lax.ppermute(send[s], "c", xor_perm(n_c, 1)) for s in range(n_y)]
    both = [keep[s].astype(F32) + other[s].astype(F32) for s in range(n_y)]
    shared = both[0]
    for s in range(1, n_y):
        shared = shared + lax.ppermute(both[s].astype(BF), "y", xor_perm(n_y, s)).astype(F32)
    own_head = heads[0].astype(F32)
    for r in range(1, n_x):
        own_head = own_head + lax.ppermute(heads[r], x_axes, xor_perm(n_x, r)).astype(F32)
    cut = shared.shape[0] // n_x
    low = shared.astype(BF)
    total = shared[:cut]
    for r in range(1, n_x):
        got = lax.ppermute(low[r * cut : (r + 1) * cut], x_axes, xor_perm(n_x, r))
        total = total + got.astype(F32)
    block = jnp.concatenate([total, own_head])
    rows = block.shape[0] // n_z
    got = lax.all_to_all(block.astype(BF).reshape(n_z, rows, ch), "z", 0, 0)
    factor = float(n_dp * tokens) ** (-0.5)
    done = (jnp.sum(got.astype(F32), axis=0) * factor).astype(BF)

    done = spread(done, "z", n_z).reshape(n_z * rows, ch)
    piece = jnp.concatenate(gather_xor(done[:cut], x_axes, n_x, i_x))
    own_head, piece = lax.optimization_barrier((done[cut:], piece))
    g_heads = [part.astype(F32) for part in gather_xor(own_head, x_axes, n_x, i_x)]
    pieces = [piece] + [lax.ppermute(piece, "y", xor_perm(n_y, s)) for s in range(1, n_y)]
    others = [lax.ppermute(p, "c", xor_perm(n_c, 1)) for p in pieces]
    pieces, others = unxor(pieces, i_y), unxor(others, i_y)
    halves = []
    for c in range(n_c):
        halves += [jnp.where(i_c == c, p, o).astype(F32) for p, o in zip(pieces, others)]
    n_ws = 9 * ch // halves[0].shape[0]
    return (
        jnp.concatenate(halves[:n_ws]).reshape(9, ch, ch),
        jnp.concatenate(halves[n_ws:]).reshape(3, ch, ch),
        *g_heads,
    )


def solution(mesh):
    frame, head, dp = (mesh.shape[a] for a in ("frame", "head", "dp"))
    sizes = (2, frame // 2, head // 2, 2, dp)
    names = ("xh", "z", "y", "c", "dp")
    fine = Mesh(mesh.devices.reshape(sizes), names)
    rows, head_axes = ("xh", "z"), ("y", "c")
    in_specs = (
        P("dp", rows, None),
        P("dp", None),
        P(),
        P(),
        P(None, head_axes),
        P(None, head_axes),
        P(None, head_axes),
        P(head_axes, None),
        P("dp", rows, None),
    )
    out_specs = (
        P(),
        P(),
        P(None, head_axes),
        P(None, head_axes),
        P(None, head_axes),
        P(head_axes, None),
    )

    def body(*args):
        return on_device(sizes, *args)

    return jax.shard_map(
        body, mesh=fine, in_specs=in_specs, out_specs=out_specs, check_vma=False
    )
```

```python
import functools

import jax
import jax.numpy as jnp
from jax import lax
from jax.experimental import pallas as pl
from jax.experimental.pallas import tpu as pltpu
from jax.sharding import Mesh, PartitionSpec as P

HD = 128
SIDE = 8
FRAME = SIDE * SIDE
NEG_FILL = -1e30
LOG2E = 1.4426950408889634
BF = jnp.bfloat16
F32 = jnp.float32


def dot(left, right):
    return jnp.dot(left, right, preferred_element_type=F32)


def contract_rows(left, right):
    return lax.dot_general(left, right, (((0,), (0,)), ((), ())), preferred_element_type=F32)


def dot_t(left, right):
    return lax.dot_general(left, right, (((1,), (1,)), ((), ())), preferred_element_type=F32)


def xor_perm(count, step):
    return [(i, i ^ step) for i in range(count)]


def unxor(parts, index):
    parts = list(parts)
    bit = 1
    while bit < len(parts):
        odd = (index & bit) != 0
        parts = [jnp.where(odd, parts[s ^ bit], parts[s]) for s in range(len(parts))]
        bit *= 2
    return parts


def gather_xor(block, axis, count, index):
    parts = [block] + [lax.ppermute(block, axis, xor_perm(count, s)) for s in range(1, count)]
    return unxor(parts, index)


def spread(block, axis, count):
    return lax.all_to_all(
        jnp.broadcast_to(block[None], (count,) + block.shape), axis, 0, 0
    )


def roll_cols(block, step):
    groups = block.reshape(-1, SIDE, block.shape[1])
    place = lax.broadcasted_iota(jnp.int32, groups.shape, 1)
    if step < 0:
        moved = jnp.where(place == 0, 0.0, pltpu.roll(groups, 1, 1))
    else:
        moved = jnp.where(place == SIDE - 1, 0.0, pltpu.roll(groups, SIDE - 1, 1))
    return moved.reshape(block.shape)


def move_rows(field, step):
    pad = jnp.zeros((field.shape[0], SIDE, field.shape[2]), field.dtype)
    if step > 0:
        return jnp.concatenate([field[:, SIDE:], pad], axis=1)
    return jnp.concatenate([pad, field[:, :-SIDE]], axis=1)


def local_kernel(
    dims,
    pos,
    ids_ref,
    *refs,
):
    n_xh, n_z, n_y, n_c, n_dp = dims
    n_x = n_xh * n_dp
    n_parts = n_y * n_c
    parts = refs[:n_parts]
    packed = refs[n_parts]
    outs = refs[n_parts + 1 : n_parts + 1 + 2 * n_y + n_x]
    send_refs, keep_refs, head_refs = outs[:n_y], outs[n_y : 2 * n_y], outs[2 * n_y :]
    (
        cols,
        slope,
        hid,
        feat,
        keys,
        values,
        gkey,
        gval,
        gf,
        e_ref,
        acc,
        heads,
        q_ref,
        g_ref,
        att_ref,
        gq_ref,
    ) = refs[n_parts + 1 + 2 * n_y + n_x :]
    tokens, ch = feat.shape
    local = q_ref.shape[0]
    rows = [9 * ch, 3 * ch, ch, ch, ch, q_ref.shape[1], local]
    starts = [sum(rows[:k]) for k in range(len(rows))]
    w_sp, w_t, w_q, w_k, w_v, w_o, up_ref = [
        packed.at[pl.ds(a, n)] for a, n in zip(starts, rows)
    ]
    my_xh, my_y, my_c, my_x = pos[0], pos[1], pos[2], pos[4]
    first = pl.multiple_of(pos[3], local)
    half = parts[0].shape[2]
    scale = HD ** (-0.5)
    n_head = n_y * n_c
    own_ids = jnp.broadcast_to(ids_ref[:, pl.ds(first, local)], (SIDE, local))
    own_ids = jnp.transpose(own_ids)[:, 0:1]

    @pl.loop(0, n_z)
    def _(z):
        for u in range(n_xh):
            for s in range(n_y):
                for t in range(n_c):
                    frame = ((my_xh ^ u) * n_z + z) * n_y + (my_y ^ s)
                    row = pl.multiple_of(frame * FRAME + (my_c ^ t) * half, half)
                    low = parts[s * n_c + t][u, z]
                    wide = low.astype(F32)
                    cols[pl.ds(row, half), 0:ch] = roll_cols(wide, -1).astype(BF)
                    cols[pl.ds(row, half), ch : 2 * ch] = low
                    cols[pl.ds(row, half), 2 * ch : 3 * ch] = roll_cols(wide, 1).astype(BF)

    edge = jnp.zeros((FRAME, ch), BF)
    hid[0:FRAME, :] = edge
    hid[tokens + FRAME : tokens + 2 * FRAME, :] = edge
    gf[0:FRAME, :] = edge
    gf[tokens + FRAME : tokens + 2 * FRAME, :] = edge
    acc[...] = jnp.zeros_like(acc)
    heads[...] = jnp.zeros_like(heads)

    chunk = min(tokens, 1024)
    n_chunk = tokens // chunk
    frames = chunk // FRAME
    @pl.loop(0, n_chunk)
    def _(i):
        row = pl.multiple_of(i * chunk, chunk)
        x = cols[pl.ds(row, chunk), :]
        mix = [
            dot(x, w_sp[a * 3 * ch : (a + 1) * 3 * ch, :]).reshape(frames, FRAME, ch)
            for a in range(3)
        ]
        pre = mix[1] + move_rows(mix[0], -1) + move_rows(mix[2], 1)
        pre = pre.reshape(chunk, ch)
        sigma = jax.nn.sigmoid(pre)
        slope[pl.ds(row, chunk), :] = sigma * (1.0 + pre * (1.0 - sigma))
        hid[pl.ds(pl.multiple_of(row + FRAME, FRAME), chunk), :] = (pre * sigma).astype(BF)

    chunk = min(tokens, 1024)
    n_chunk = tokens // chunk
    @pl.loop(0, n_chunk)
    def _(i):
        row = pl.multiple_of(i * chunk, chunk)
        total = dot(hid[pl.ds(row, chunk), :], w_t[0:ch, :])
        for d in range(1, 3):
            at = pl.multiple_of(row + d * FRAME, FRAME)
            total = total + dot(hid[pl.ds(at, chunk), :], w_t[d * ch : (d + 1) * ch, :])
        low = total.astype(BF)
        feat[pl.ds(row, chunk), :] = low
        keys[pl.ds(row, chunk), :] = dot(low, w_k[...]).astype(BF)
        values[pl.ds(row, chunk), :] = dot(low, w_v[...]).astype(BF)

    q_ref[...] = dot(feat[pl.ds(first, local), :], w_q[...]).astype(BF)
    g_ref[...] = dot_t(up_ref[...], w_o[...]).astype(BF)

    chunk = min(tokens, 4096)
    n_chunk = tokens // chunk
    def fold(block, join):
        out = block[:, 0:HD]
        for k in range(1, block.shape[1] // HD):
            out = join(out, block[:, k * HD : (k + 1) * HD])
        return out

    for h in range(q_ref.shape[1] // HD):
        sel = slice(h * HD, (h + 1) * HD)

        def raw(i, top):
            row = pl.multiple_of(i * chunk, chunk)
            s = dot_t(q_ref[:, sel], keys[pl.ds(row, chunk), sel])
            s = jnp.where(ids_ref[:, pl.ds(row, chunk)] <= own_ids, s, NEG_FILL)
            e_ref[:, pl.ds(row, chunk)] = s
            return jnp.maximum(top, fold(s, jnp.maximum))

        top = lax.fori_loop(0, n_chunk, raw, jnp.full((local, HD), NEG_FILL, F32))
        top = jnp.max(top, axis=1, keepdims=True)

        def forward(i, carry):
            total, out = carry
            row = pl.multiple_of(i * chunk, chunk)
            e = jnp.exp2((e_ref[:, pl.ds(row, chunk)] - top) * (scale * LOG2E))
            e_ref[:, pl.ds(row, chunk)] = e
            total = total + fold(e, jnp.add)
            return total, out + dot(e.astype(BF), values[pl.ds(row, chunk), sel])

        zero = jnp.zeros((local, HD), F32)
        total, out = lax.fori_loop(0, n_chunk, forward, (zero, zero))
        inv = 1.0 / jnp.sum(total, axis=1, keepdims=True)
        att = (out * inv).astype(BF)
        att_ref[:, sel] = att
        delta = jnp.sum(g_ref[:, sel].astype(F32) * att.astype(F32), axis=1, keepdims=True)

        def backward(i, gq):
            row = pl.multiple_of(i * chunk, chunk)
            p = e_ref[:, pl.ds(row, chunk)] * inv
            g = g_ref[:, sel]
            k = keys[pl.ds(row, chunk), sel]
            ds = (p * (dot_t(g, values[pl.ds(row, chunk), sel]) - delta)).astype(BF)
            gkey[pl.ds(row, chunk), sel] = (contract_rows(ds, q_ref[:, sel]) * scale).astype(BF)
            gval[pl.ds(row, chunk), sel] = contract_rows(p.astype(BF), g).astype(BF)
            return gq + dot(ds, k)

        gq = lax.fori_loop(0, n_chunk, backward, zero)
        gq_ref[:, sel] = (gq * scale).astype(BF)

    chunk = min(tokens, 2048)
    n_chunk = tokens // chunk
    @pl.loop(0, n_chunk)
    def _(i):
        row = pl.multiple_of(i * chunk, chunk)
        gk, gv = gkey[pl.ds(row, chunk), :], gval[pl.ds(row, chunk), :]
        f = feat[pl.ds(row, chunk), :]
        at = pl.multiple_of(row + FRAME, FRAME)
        gf[pl.ds(at, chunk), :] = (dot_t(gk, w_k[...]) + dot_t(gv, w_v[...])).astype(BF)
        heads[ch : 2 * ch, :] += contract_rows(f, gk)
        heads[2 * ch : 3 * ch, :] += contract_rows(f, gv)

    own = pl.ds(first, local)
    up = up_ref[...]
    total = dot_t(gkey[own, :], w_k[...]) + dot_t(gval[own, :], w_v[...])
    total = total + dot_t(gq_ref[...], w_q[...]) + up.astype(F32) * (1.0 / n_head)
    gf[pl.ds(pl.multiple_of(first + FRAME, FRAME), local), :] = total.astype(BF)
    heads[0:ch, :] = contract_rows(feat[own, :], gq_ref[...])
    heads[3 * ch : 4 * ch, :] = contract_rows(att_ref[...], up)

    chunk = min(tokens, 1024)
    n_chunk = tokens // chunk
    frames = chunk // FRAME
    @pl.loop(0, n_chunk)
    def _(i):
        row = pl.multiple_of(i * chunk, chunk)
        here = gf[pl.ds(pl.multiple_of(row + FRAME, FRAME), chunk), :]
        back = jnp.zeros((chunk, ch), F32)
        for d in range(3):
            at = pl.multiple_of(row + d * FRAME, FRAME)
            acc[(9 + d) * ch : (10 + d) * ch, :] += contract_rows(hid[pl.ds(at, chunk), :], here)
            at = pl.multiple_of(row + (2 - d) * FRAME, FRAME)
            back = back + dot_t(gf[pl.ds(at, chunk), :], w_t[d * ch : (d + 1) * ch, :])
        gp = (back * slope[pl.ds(row, chunk), :]).reshape(frames, FRAME, ch)
        x = cols[pl.ds(row, chunk), :]
        for a in range(3):
            moved = gp if a == 1 else move_rows(gp, 1 - a)
            moved = moved.reshape(chunk, ch).astype(BF)
            acc[a * 3 * ch : (a + 1) * 3 * ch, :] += contract_rows(x, moved)

    rows = keep_refs[0].shape[0]
    sub = rows // n_x
    for s in range(n_y):
        for r in range(n_x):
            at = (my_y ^ s) * rows + (my_x ^ r) * sub
            here = slice(r * sub, (r + 1) * sub)
            for ref, which in ((send_refs[s], 1 - my_c), (keep_refs[s], my_c)):
                row = pl.multiple_of(which * (n_y * rows) + at, SIDE)
                ref[here, :] = acc[pl.ds(row, sub), :].astype(BF)
    for r in range(n_x):
        head_refs[r][...] = heads[pl.ds(pl.multiple_of((my_x ^ r) * ch, ch), ch), :].astype(BF)


def local_terms(sizes, pos, ids, parts, weights, up):
    n_xh, n_z, n_y, n_c, n_dp = sizes
    n_x = n_xh * n_dp
    local, ch = up.shape
    tokens = local * n_xh * n_z
    wide = weights[2].shape[1]
    block = 12 * ch // (n_c * n_y)
    vm = pl.BlockSpec(memory_space=pltpu.VMEM)
    packed = jnp.concatenate([*weights, up])
    ids = ids.astype(F32)
    n_in = 2 + len(parts)
    shapes = [(block, ch)] * (2 * n_y) + [(4 * ch // n_x, ch)] * n_x
    out = pl.pallas_call(
        functools.partial(local_kernel, sizes),
        name="local_terms",
        out_shape=[jax.ShapeDtypeStruct(s, BF) for s in shapes],
        in_specs=[pl.BlockSpec(memory_space=pltpu.SMEM)] + [vm] * n_in,
        out_specs=[vm] * len(shapes),
        scratch_shapes=[
            pltpu.VMEM((tokens, 3 * ch), BF),
            pltpu.VMEM((tokens, ch), F32),
            pltpu.VMEM((tokens + 2 * FRAME, ch), BF),
            pltpu.VMEM((tokens, ch), BF),
            pltpu.VMEM((tokens, wide), BF),
            pltpu.VMEM((tokens, wide), BF),
            pltpu.VMEM((tokens, wide), BF),
            pltpu.VMEM((tokens, wide), BF),
            pltpu.VMEM((tokens + 2 * FRAME, ch), BF),
            pltpu.VMEM((local, tokens), F32),
            pltpu.VMEM((12 * ch, ch), F32),
            pltpu.VMEM((4 * ch, ch), F32),
            pltpu.VMEM((local, wide), BF),
            pltpu.VMEM((local, wide), BF),
            pltpu.VMEM((local, wide), BF),
            pltpu.VMEM((local, wide), BF),
        ],
        compiler_params=pltpu.CompilerParams(vmem_limit_bytes=42 * 2**20),
        cost_estimate=pl.CostEstimate(
            flops=24 * 10**9, transcendentals=2 * local * tokens, bytes_accessed=12 * 2**20
        ),
    )(pos, ids, *parts, packed)
    return out[:n_y], out[n_y : 2 * n_y], out[2 * n_y :]


def place_kernel(pos, *refs):
    *blocks, first_ref, second_ref = refs
    n_y = len(blocks) // 2
    rows = blocks[0].shape[0]
    n_first = first_ref.shape[0] // rows
    for k, ref in enumerate(blocks):
        which = pos[2] if k < n_y else 1 - pos[2]
        at = which * n_y + (pos[1] ^ (k % n_y))

        @pl.when(at < n_first)
        def _():
            row = pl.multiple_of(at * rows, rows)
            first_ref[pl.ds(row, rows), :] = ref[...].astype(F32)

        @pl.when(at >= n_first)
        def _():
            row = pl.multiple_of((at - n_first) * rows, rows)
            second_ref[pl.ds(row, rows), :] = ref[...].astype(F32)


def place(pos, pieces, others, n_first):
    rows, ch = pieces[0].shape
    total = rows * 2 * len(pieces)
    vm = pl.BlockSpec(memory_space=pltpu.VMEM)
    return pl.pallas_call(
        place_kernel,
        name="place",
        out_shape=(
            jax.ShapeDtypeStruct((n_first, ch), F32),
            jax.ShapeDtypeStruct((total - n_first, ch), F32),
        ),
        in_specs=[pl.BlockSpec(memory_space=pltpu.SMEM)] + [vm] * (2 * len(pieces)),
        out_specs=(vm, vm),
        compiler_params=pltpu.CompilerParams(vmem_limit_bytes=16 * 2**20),
        cost_estimate=pl.CostEstimate(
            flops=0, transcendentals=0, bytes_accessed=6 * total * ch
        ),
    )(pos, *pieces, *others)


def on_device(sizes, clip, block_ids, w_spatial, w_temporal, w_query, w_key, w_value, w_out, cotangent):
    n_xh, n_z, n_y, n_c, n_dp = sizes
    i_xh, i_y, i_c, i_dp = (lax.axis_index(a) for a in ("xh", "y", "c", "dp"))
    i_x = i_xh * n_dp + i_dp
    n_head = n_y * n_c
    n_frame = n_xh * n_z
    own_clip = clip[0]
    upstream = cotangent[0]
    ids = block_ids[0]
    local, ch = own_clip.shape
    tokens = local * n_frame

    piece = local // n_head
    mine = lax.dynamic_slice_in_dim(own_clip, lax.axis_index(("y", "c")) * piece, piece)
    part = spread(mine, "z", n_z)
    part = jnp.stack([part, lax.ppermute(part, "xh", xor_perm(n_xh, 1))])
    parts = []
    for s in range(n_y):
        block = part if s == 0 else lax.ppermute(part, "y", xor_perm(n_y, s))
        parts += [block, lax.ppermute(block, "c", xor_perm(n_c, 1))]

    first = lax.axis_index(("xh", "z")) * local
    pos = jnp.stack([i_xh, i_y, i_c, first, i_x]).astype(jnp.int32)
    weights = (
        w_spatial.reshape(9 * ch, ch),
        w_temporal.reshape(3 * ch, ch),
        w_query,
        w_key,
        w_value,
        w_out,
    )
    send, keep, heads = local_terms(sizes, pos, ids[None], parts, weights, upstream)

    n_x = n_xh * n_dp
    x_axes = ("xh", "dp")
    other = [lax.ppermute(send[s], "c", xor_perm(n_c, 1)) for s in range(n_y)]
    both = [keep[s].astype(F32) + other[s].astype(F32) for s in range(n_y)]
    shared = both[0]
    for s in range(1, n_y):
        shared = shared + lax.ppermute(both[s].astype(BF), "y", xor_perm(n_y, s)).astype(F32)
    own_head = heads[0].astype(F32)
    for r in range(1, n_x):
        own_head = own_head + lax.ppermute(heads[r], x_axes, xor_perm(n_x, r)).astype(F32)
    cut = shared.shape[0] // n_x
    low = shared.astype(BF)
    total = shared[:cut]
    for r in range(1, n_x):
        got = lax.ppermute(low[r * cut : (r + 1) * cut], x_axes, xor_perm(n_x, r))
        total = total + got.astype(F32)
    block = jnp.concatenate([total, own_head])
    rows = block.shape[0] // n_z
    got = lax.all_to_all(block.astype(BF).reshape(n_z, rows, ch), "z", 0, 0)
    factor = float(n_dp * tokens) ** (-0.5)
    done = (jnp.sum(got.astype(F32), axis=0) * factor).astype(BF)

    done = spread(done, "z", n_z).reshape(n_z * rows, ch)
    done = gather_xor(done, x_axes, n_x, i_x)
    g_heads = [part[cut:].astype(F32) for part in done]
    piece = jnp.concatenate([part[:cut] for part in done])
    pieces = [piece] + [lax.ppermute(piece, "y", xor_perm(n_y, s)) for s in range(1, n_y)]
    others = [lax.ppermute(p, "c", xor_perm(n_c, 1)) for p in pieces]
    g_ws, g_wt = place(pos, pieces, others, 9 * ch)
    return (g_ws.reshape(9, ch, ch), g_wt.reshape(3, ch, ch), *g_heads)


def solution(mesh):
    frame, head, dp = (mesh.shape[a] for a in ("frame", "head", "dp"))
    sizes = (2, frame // 2, head // 2, 2, dp)
    names = ("xh", "z", "y", "c", "dp")
    fine = Mesh(mesh.devices.reshape(sizes), names)
    rows, head_axes = ("xh", "z"), ("y", "c")
    in_specs = (
        P("dp", rows, None),
        P("dp", None),
        P(),
        P(),
        P(None, head_axes),
        P(None, head_axes),
        P(None, head_axes),
        P(head_axes, None),
        P("dp", rows, None),
    )
    out_specs = (
        P(),
        P(),
        P(None, head_axes),
        P(None, head_axes),
        P(None, head_axes),
        P(head_axes, None),
    )

    def body(*args):
        return on_device(sizes, *args)

    return jax.shard_map(
        body, mesh=fine, in_specs=in_specs, out_specs=out_specs, check_vma=False
    )
```

```python
import functools

import jax
import jax.numpy as jnp
from jax import lax
from jax.experimental import pallas as pl
from jax.experimental.pallas import tpu as pltpu
from jax.sharding import Mesh, PartitionSpec as P

HD = 128
SIDE = 8
FRAME = SIDE * SIDE
NEG_FILL = -1e30
LOG2E = 1.4426950408889634
BF = jnp.bfloat16
F32 = jnp.float32


def dot(left, right):
    return jnp.dot(left, right, preferred_element_type=F32)


def contract_rows(left, right):
    return lax.dot_general(left, right, (((0,), (0,)), ((), ())), preferred_element_type=F32)


def dot_t(left, right):
    return lax.dot_general(left, right, (((1,), (1,)), ((), ())), preferred_element_type=F32)


def xor_perm(count, step):
    return [(i, i ^ step) for i in range(count)]


def unxor(parts, index):
    parts = list(parts)
    bit = 1
    while bit < len(parts):
        odd = (index & bit) != 0
        parts = [jnp.where(odd, parts[s ^ bit], parts[s]) for s in range(len(parts))]
        bit *= 2
    return parts


def gather_xor(block, axis, count, index):
    parts = [block] + [lax.ppermute(block, axis, xor_perm(count, s)) for s in range(1, count)]
    return unxor(parts, index)


def spread(block, axis, count):
    return lax.all_to_all(
        jnp.broadcast_to(block[None], (count,) + block.shape), axis, 0, 0
    )


def roll_cols(block, step):
    groups = block.reshape(-1, SIDE, block.shape[1])
    place = lax.broadcasted_iota(jnp.int32, groups.shape, 1)
    if step < 0:
        moved = jnp.where(place == 0, 0.0, pltpu.roll(groups, 1, 1))
    else:
        moved = jnp.where(place == SIDE - 1, 0.0, pltpu.roll(groups, SIDE - 1, 1))
    return moved.reshape(block.shape)


def move_rows(field, step):
    pad = jnp.zeros((field.shape[0], SIDE, field.shape[2]), field.dtype)
    if step > 0:
        return jnp.concatenate([field[:, SIDE:], pad], axis=1)
    return jnp.concatenate([pad, field[:, :-SIDE]], axis=1)


def local_kernel(
    dims,
    pos,
    ids_ref,
    *refs,
):
    n_xh, n_z, n_y, n_c, n_dp = dims
    n_x = n_xh * n_dp
    n_parts = n_y * n_c
    parts = refs[:n_parts]
    packed = refs[n_parts]
    outs = refs[n_parts + 1 : n_parts + 1 + 2 * n_y + n_x]
    send_refs, keep_refs, head_refs = outs[:n_y], outs[n_y : 2 * n_y], outs[2 * n_y :]
    (
        cols,
        slope,
        hid,
        feat,
        keys,
        values,
        gkey,
        gval,
        gf,
        e_ref,
        acc,
        heads,
        q_ref,
        g_ref,
        att_ref,
        gq_ref,
    ) = refs[n_parts + 1 + 2 * n_y + n_x :]
    tokens, ch = feat.shape
    local = q_ref.shape[0]
    rows = [9 * ch, 3 * ch, ch, ch, ch, q_ref.shape[1], local]
    starts = [sum(rows[:k]) for k in range(len(rows))]
    w_sp, w_t, w_q, w_k, w_v, w_o, up_ref = [
        packed.at[pl.ds(a, n)] for a, n in zip(starts, rows)
    ]
    my_xh, my_y, my_c, my_x = pos[0], pos[1], pos[2], pos[4]
    first = pl.multiple_of(pos[3], local)
    half = parts[0].shape[2]
    scale = HD ** (-0.5)
    n_head = n_y * n_c
    own_ids = jnp.broadcast_to(ids_ref[:, pl.ds(first, local)], (SIDE, local))
    own_ids = jnp.transpose(own_ids)[:, 0:1]

    @pl.loop(0, n_z)
    def _(z):
        for u in range(n_xh):
            for s in range(n_y):
                for t in range(n_c):
                    frame = ((my_xh ^ u) * n_z + z) * n_y + (my_y ^ s)
                    row = pl.multiple_of(frame * FRAME + (my_c ^ t) * half, half)
                    low = parts[s * n_c + t][u, z]
                    wide = low.astype(F32)
                    cols[pl.ds(row, half), 0:ch] = roll_cols(wide, -1).astype(BF)
                    cols[pl.ds(row, half), ch : 2 * ch] = low
                    cols[pl.ds(row, half), 2 * ch : 3 * ch] = roll_cols(wide, 1).astype(BF)

    edge = jnp.zeros((FRAME, ch), BF)
    hid[0:FRAME, :] = edge
    hid[tokens + FRAME : tokens + 2 * FRAME, :] = edge
    gf[0:FRAME, :] = edge
    gf[tokens + FRAME : tokens + 2 * FRAME, :] = edge
    acc[...] = jnp.zeros_like(acc)
    heads[...] = jnp.zeros_like(heads)

    chunk = min(tokens, 1024)
    n_chunk = tokens // chunk
    frames = chunk // FRAME
    @pl.loop(0, n_chunk)
    def _(i):
        row = pl.multiple_of(i * chunk, chunk)
        x = cols[pl.ds(row, chunk), :]
        mix = [
            dot(x, w_sp[a * 3 * ch : (a + 1) * 3 * ch, :]).reshape(frames, FRAME, ch)
            for a in range(3)
        ]
        pre = mix[1] + move_rows(mix[0], -1) + move_rows(mix[2], 1)
        pre = pre.reshape(chunk, ch)
        sigma = jax.nn.sigmoid(pre)
        slope[pl.ds(row, chunk), :] = sigma * (1.0 + pre * (1.0 - sigma))
        hid[pl.ds(pl.multiple_of(row + FRAME, FRAME), chunk), :] = (pre * sigma).astype(BF)

    chunk = min(tokens, 2048)
    n_chunk = tokens // chunk
    @pl.loop(0, n_chunk)
    def _(i):
        row = pl.multiple_of(i * chunk, chunk)
        total = dot(hid[pl.ds(row, chunk), :], w_t[0:ch, :])
        for d in range(1, 3):
            at = pl.multiple_of(row + d * FRAME, FRAME)
            total = total + dot(hid[pl.ds(at, chunk), :], w_t[d * ch : (d + 1) * ch, :])
        low = total.astype(BF)
        feat[pl.ds(row, chunk), :] = low
        keys[pl.ds(row, chunk), :] = dot(low, w_k[...]).astype(BF)
        values[pl.ds(row, chunk), :] = dot(low, w_v[...]).astype(BF)

    q_ref[...] = dot(feat[pl.ds(first, local), :], w_q[...]).astype(BF)
    g_ref[...] = dot_t(up_ref[...], w_o[...]).astype(BF)

    chunk = min(tokens, 4096)
    n_chunk = tokens // chunk
    def fold(block, join):
        out = block[:, 0:HD]
        for k in range(1, block.shape[1] // HD):
            out = join(out, block[:, k * HD : (k + 1) * HD])
        return out

    for h in range(q_ref.shape[1] // HD):
        sel = slice(h * HD, (h + 1) * HD)

        def raw(i, top):
            row = pl.multiple_of(i * chunk, chunk)
            s = dot_t(q_ref[:, sel], keys[pl.ds(row, chunk), sel])
            s = jnp.where(ids_ref[:, pl.ds(row, chunk)] <= own_ids, s, NEG_FILL)
            e_ref[:, pl.ds(row, chunk)] = s
            return jnp.maximum(top, fold(s, jnp.maximum))

        top = lax.fori_loop(0, n_chunk, raw, jnp.full((local, HD), NEG_FILL, F32))
        top = jnp.max(top, axis=1, keepdims=True)

        def forward(i, carry):
            total, out = carry
            row = pl.multiple_of(i * chunk, chunk)
            e = jnp.exp2((e_ref[:, pl.ds(row, chunk)] - top) * (scale * LOG2E))
            e_ref[:, pl.ds(row, chunk)] = e
            total = total + fold(e, jnp.add)
            return total, out + dot(e.astype(BF), values[pl.ds(row, chunk), sel])

        zero = jnp.zeros((local, HD), F32)
        total, out = lax.fori_loop(0, n_chunk, forward, (zero, zero))
        inv = 1.0 / jnp.sum(total, axis=1, keepdims=True)
        att = (out * inv).astype(BF)
        att_ref[:, sel] = att
        delta = jnp.sum(g_ref[:, sel].astype(F32) * att.astype(F32), axis=1, keepdims=True)

        def backward(i, gq):
            row = pl.multiple_of(i * chunk, chunk)
            p = e_ref[:, pl.ds(row, chunk)] * inv
            g = g_ref[:, sel]
            k = keys[pl.ds(row, chunk), sel]
            ds = (p * (dot_t(g, values[pl.ds(row, chunk), sel]) - delta)).astype(BF)
            gkey[pl.ds(row, chunk), sel] = (contract_rows(ds, q_ref[:, sel]) * scale).astype(BF)
            gval[pl.ds(row, chunk), sel] = contract_rows(p.astype(BF), g).astype(BF)
            return gq + dot(ds, k)

        gq = lax.fori_loop(0, n_chunk, backward, zero)
        gq_ref[:, sel] = (gq * scale).astype(BF)

    chunk = min(tokens, 2048)
    n_chunk = tokens // chunk
    @pl.loop(0, n_chunk)
    def _(i):
        row = pl.multiple_of(i * chunk, chunk)
        gk, gv = gkey[pl.ds(row, chunk), :], gval[pl.ds(row, chunk), :]
        f = feat[pl.ds(row, chunk), :]
        at = pl.multiple_of(row + FRAME, FRAME)
        gf[pl.ds(at, chunk), :] = (dot_t(gk, w_k[...]) + dot_t(gv, w_v[...])).astype(BF)
        heads[ch : 2 * ch, :] += contract_rows(f, gk)
        heads[2 * ch : 3 * ch, :] += contract_rows(f, gv)

    own = pl.ds(first, local)
    up = up_ref[...]
    total = dot_t(gkey[own, :], w_k[...]) + dot_t(gval[own, :], w_v[...])
    total = total + dot_t(gq_ref[...], w_q[...]) + up.astype(F32) * (1.0 / n_head)
    gf[pl.ds(pl.multiple_of(first + FRAME, FRAME), local), :] = total.astype(BF)
    heads[0:ch, :] = contract_rows(feat[own, :], gq_ref[...])
    heads[3 * ch : 4 * ch, :] = contract_rows(att_ref[...], up)

    chunk = min(tokens, 1024)
    n_chunk = tokens // chunk
    frames = chunk // FRAME
    @pl.loop(0, n_chunk)
    def _(i):
        row = pl.multiple_of(i * chunk, chunk)
        here = gf[pl.ds(pl.multiple_of(row + FRAME, FRAME), chunk), :]
        back = jnp.zeros((chunk, ch), F32)
        for d in range(3):
            at = pl.multiple_of(row + d * FRAME, FRAME)
            acc[(9 + d) * ch : (10 + d) * ch, :] += contract_rows(hid[pl.ds(at, chunk), :], here)
            at = pl.multiple_of(row + (2 - d) * FRAME, FRAME)
            back = back + dot_t(gf[pl.ds(at, chunk), :], w_t[d * ch : (d + 1) * ch, :])
        gp = (back * slope[pl.ds(row, chunk), :]).reshape(frames, FRAME, ch)
        x = cols[pl.ds(row, chunk), :]
        for a in range(3):
            moved = gp if a == 1 else move_rows(gp, 1 - a)
            moved = moved.reshape(chunk, ch).astype(BF)
            acc[a * 3 * ch : (a + 1) * 3 * ch, :] += contract_rows(x, moved)

    rows = keep_refs[0].shape[0]
    sub = rows // n_x
    for s in range(n_y):
        for r in range(n_x):
            at = (my_y ^ s) * rows + (my_x ^ r) * sub
            here = slice(r * sub, (r + 1) * sub)
            for ref, which in ((send_refs[s], 1 - my_c), (keep_refs[s], my_c)):
                row = pl.multiple_of(which * (n_y * rows) + at, SIDE)
                ref[here, :] = acc[pl.ds(row, sub), :].astype(BF)
    for r in range(n_x):
        head_refs[r][...] = heads[pl.ds(pl.multiple_of((my_x ^ r) * ch, ch), ch), :].astype(BF)


def local_terms(sizes, pos, ids, parts, weights, up):
    n_xh, n_z, n_y, n_c, n_dp = sizes
    n_x = n_xh * n_dp
    local, ch = up.shape
    tokens = local * n_xh * n_z
    wide = weights[2].shape[1]
    block = 12 * ch // (n_c * n_y)
    vm = pl.BlockSpec(memory_space=pltpu.VMEM)
    packed = jnp.concatenate([*weights, up])
    ids = ids.astype(F32)
    n_in = 2 + len(parts)
    shapes = [(block, ch)] * (2 * n_y) + [(4 * ch // n_x, ch)] * n_x
    out = pl.pallas_call(
        functools.partial(local_kernel, sizes),
        name="local_terms",
        out_shape=[jax.ShapeDtypeStruct(s, BF) for s in shapes],
        in_specs=[pl.BlockSpec(memory_space=pltpu.SMEM)] + [vm] * n_in,
        out_specs=[vm] * len(shapes),
        scratch_shapes=[
            pltpu.VMEM((tokens, 3 * ch), BF),
            pltpu.VMEM((tokens, ch), F32),
            pltpu.VMEM((tokens + 2 * FRAME, ch), BF),
            pltpu.VMEM((tokens, ch), BF),
            pltpu.VMEM((tokens, wide), BF),
            pltpu.VMEM((tokens, wide), BF),
            pltpu.VMEM((tokens, wide), BF),
            pltpu.VMEM((tokens, wide), BF),
            pltpu.VMEM((tokens + 2 * FRAME, ch), BF),
            pltpu.VMEM((local, tokens), F32),
            pltpu.VMEM((12 * ch, ch), F32),
            pltpu.VMEM((4 * ch, ch), F32),
            pltpu.VMEM((local, wide), BF),
            pltpu.VMEM((local, wide), BF),
            pltpu.VMEM((local, wide), BF),
            pltpu.VMEM((local, wide), BF),
        ],
        compiler_params=pltpu.CompilerParams(vmem_limit_bytes=42 * 2**20),
        cost_estimate=pl.CostEstimate(
            flops=24 * 10**9, transcendentals=2 * local * tokens, bytes_accessed=12 * 2**20
        ),
    )(pos, ids, *parts, packed)
    return out[:n_y], out[n_y : 2 * n_y], out[2 * n_y :]


def place_kernel(pos, *refs):
    *blocks, first_ref, second_ref = refs
    n_y = len(blocks) // 2
    rows = blocks[0].shape[0]
    n_first = first_ref.shape[0] // rows
    for k, ref in enumerate(blocks):
        which = pos[2] if k < n_y else 1 - pos[2]
        at = which * n_y + (pos[1] ^ (k % n_y))

        @pl.when(at < n_first)
        def _():
            row = pl.multiple_of(at * rows, rows)
            first_ref[pl.ds(row, rows), :] = ref[...].astype(F32)

        @pl.when(at >= n_first)
        def _():
            row = pl.multiple_of((at - n_first) * rows, rows)
            second_ref[pl.ds(row, rows), :] = ref[...].astype(F32)


def place(pos, pieces, others, n_first):
    rows, ch = pieces[0].shape
    total = rows * 2 * len(pieces)
    vm = pl.BlockSpec(memory_space=pltpu.VMEM)
    return pl.pallas_call(
        place_kernel,
        name="place",
        out_shape=(
            jax.ShapeDtypeStruct((n_first, ch), F32),
            jax.ShapeDtypeStruct((total - n_first, ch), F32),
        ),
        in_specs=[pl.BlockSpec(memory_space=pltpu.SMEM)] + [vm] * (2 * len(pieces)),
        out_specs=(vm, vm),
        compiler_params=pltpu.CompilerParams(vmem_limit_bytes=16 * 2**20),
        cost_estimate=pl.CostEstimate(
            flops=0, transcendentals=0, bytes_accessed=6 * total * ch
        ),
    )(pos, *pieces, *others)


def on_device(sizes, clip, block_ids, w_spatial, w_temporal, w_query, w_key, w_value, w_out, cotangent):
    n_xh, n_z, n_y, n_c, n_dp = sizes
    i_xh, i_y, i_c, i_dp = (lax.axis_index(a) for a in ("xh", "y", "c", "dp"))
    i_x = i_xh * n_dp + i_dp
    n_head = n_y * n_c
    n_frame = n_xh * n_z
    own_clip = clip[0]
    upstream = cotangent[0]
    ids = block_ids[0]
    local, ch = own_clip.shape
    tokens = local * n_frame

    piece = local // n_head
    mine = lax.dynamic_slice_in_dim(own_clip, lax.axis_index(("y", "c")) * piece, piece)
    part = spread(mine, "z", n_z)
    part = jnp.stack([part, lax.ppermute(part, "xh", xor_perm(n_xh, 1))])
    parts = []
    for s in range(n_y):
        block = part if s == 0 else lax.ppermute(part, "y", xor_perm(n_y, s))
        parts += [block, lax.ppermute(block, "c", xor_perm(n_c, 1))]

    first = lax.axis_index(("xh", "z")) * local
    pos = jnp.stack([i_xh, i_y, i_c, first, i_x]).astype(jnp.int32)
    weights = (
        w_spatial.reshape(9 * ch, ch),
        w_temporal.reshape(3 * ch, ch),
        w_query,
        w_key,
        w_value,
        w_out,
    )
    send, keep, heads = local_terms(sizes, pos, ids[None], parts, weights, upstream)

    n_x = n_xh * n_dp
    x_axes = ("xh", "dp")
    other = [lax.ppermute(send[s], "c", xor_perm(n_c, 1)) for s in range(n_y)]
    both = [keep[s].astype(F32) + other[s].astype(F32) for s in range(n_y)]
    shared = both[0]
    for s in range(1, n_y):
        shared = shared + lax.ppermute(both[s].astype(BF), "y", xor_perm(n_y, s)).astype(F32)
    own_head = heads[0].astype(F32)
    for r in range(1, n_x):
        own_head = own_head + lax.ppermute(heads[r], x_axes, xor_perm(n_x, r)).astype(F32)
    cut = shared.shape[0] // n_x
    low = shared.astype(BF)
    total = shared[:cut]
    for r in range(1, n_x):
        got = lax.ppermute(low[r * cut : (r + 1) * cut], x_axes, xor_perm(n_x, r))
        total = total + got.astype(F32)
    block = jnp.concatenate([total, own_head])
    rows = block.shape[0] // n_z
    got = lax.all_to_all(block.astype(BF).reshape(n_z, rows, ch), "z", 0, 0)
    factor = float(n_dp * tokens) ** (-0.5)
    done = (jnp.sum(got.astype(F32), axis=0) * factor).astype(BF)

    done = spread(done, "z", n_z).reshape(n_z * rows, ch)
    done = gather_xor(done, x_axes, n_x, i_x)
    g_heads = [part[cut:].astype(F32) for part in done]
    piece = jnp.concatenate([part[:cut] for part in done])
    pieces = [piece] + [lax.ppermute(piece, "y", xor_perm(n_y, s)) for s in range(1, n_y)]
    others = [lax.ppermute(p, "c", xor_perm(n_c, 1)) for p in pieces]
    g_ws, g_wt = place(pos, pieces, others, 9 * ch)
    return (g_ws.reshape(9, ch, ch), g_wt.reshape(3, ch, ch), *g_heads)


def solution(mesh):
    frame, head, dp = (mesh.shape[a] for a in ("frame", "head", "dp"))
    sizes = (2, frame // 2, head // 2, 2, dp)
    names = ("xh", "z", "y", "c", "dp")
    fine = Mesh(mesh.devices.reshape(sizes), names)
    rows, head_axes = ("xh", "z"), ("y", "c")
    in_specs = (
        P("dp", rows, None),
        P("dp", None),
        P(),
        P(),
        P(None, head_axes),
        P(None, head_axes),
        P(None, head_axes),
        P(head_axes, None),
        P("dp", rows, None),
    )
    out_specs = (
        P(),
        P(),
        P(None, head_axes),
        P(None, head_axes),
        P(None, head_axes),
        P(head_axes, None),
    )

    def body(*args):
        return on_device(sizes, *args)

    return jax.shard_map(
        body, mesh=fine, in_specs=in_specs, out_specs=out_specs, check_vma=False
    )
```
